128 devices in a mesh: replica: 4 (over y_hi, core), fsdp: 32 (over y_lo, z, x).
Axes of the slice: x: 4, y: 4 (y_hi: 2, y_lo: 2; y = y_hi * 2 + y_lo), z: 4, core: 2. Of those that a mesh axis runs over, the one named last changes fastest.
Arguments:
- layer_input: bfloat16 [4, 16384, 4096], P('replica', 'fsdp'), may hold values from -36 to 36, as said below
- norm_gain: bfloat16 [4, 4096], P('replica', 'fsdp'), may hold values from 0.099609375 to 1.8984375
- kv_weight: bfloat16 [4, 4096, 1024], P('replica', 'fsdp'), may hold values from -0.09375 to 0.09375
- kv_cotangent: bfloat16 [4, 16384, 1024], P('replica', 'fsdp'), may hold values from -6 to 6
- pseudo_grad: float32 [4, 12288, 1024], P('replica', 'fsdp'), may hold values from -6 to 6
- outer_momentum: float32 [12288, 1024], P('fsdp'), may hold values from -6 to 6
- global_params: float32 [12288, 1024], P('fsdp'), may hold values from -6 to 6
- local_params: bfloat16 [4, 12288, 1024], P('replica', 'fsdp'), may hold values from -6 to 6
Outputs:
- kv_out: bfloat16 [4, 16384, 1024], P('replica', 'fsdp')
- input_grad: bfloat16 [4, 16384, 4096], P('replica', 'fsdp')
- kv_weight_grad: float32 [4, 4096, 1024], P('replica', 'fsdp')
- gain_grad: float32 [4, 4096], P('replica', 'fsdp')
- momentum_new: float32 [12288, 1024], P('fsdp')
- global_new: float32 [12288, 1024], P('fsdp')
- local_new: bfloat16 [4, 12288, 1024], P('replica', 'fsdp')
The draws below stay inside these ranges and needn't reach their ends.
Inputs may be any that keep to these rules, and one draw needn't show every extreme that they name: `layer_input`: activations of the residual stream.
All inputs are finite; a program needn't handle non-finite values.
Results may differ from the reference program's by a relative error of at most 0.0049.
Values may be sent and summed in bfloat16 or wider, within the bound.
A program may use at most 128 MiB of HBM per device.

```python
import math
import jax
import jax.numpy as jnp
from jax import lax

D = 4096
HEAD = 128
KVW = 512
SEQ_LEN = 4096
TOK_DEV = 512
TOKENS = 16384
FCOLS = 1024
FROWS = 12288
N_REPLICA = 4
N_FSDP = 32


def draw_layer_input(key, part):
    first, second, third = jax.random.split(key, 3)
    shape = (N_REPLICA, TOKENS, D)
    base = jnp.clip(jax.random.normal(first, shape, jnp.float32), -4.0, 4.0)
    row_scale = jnp.exp(jax.random.uniform(second, (N_REPLICA, TOKENS, 1), jnp.float32, math.log(0.3), math.log(3.0)))
    col_scale = jnp.exp(jax.random.uniform(third, (N_REPLICA, 1, D), jnp.float32, math.log(0.3), math.log(3.0)))
    return (base * row_scale * col_scale).astype(jnp.bfloat16)


def shard_levels(rng, extent, shards, least, largest):
    def one(axis_at, shards_of):
        heights = jax.random.uniform(jax.random.fold_in(jax.random.fold_in(rng, 6), axis_at), (shards_of,), jnp.float32, least / len(shards), largest / len(shards))
        return jnp.repeat(jnp.exp(heights), extent[axis_at] // shards_of).reshape((-1,) + (1,) * (len(extent) - axis_at - 1))

    factor_of = one(*shards[0])
    for cut in shards[1:]:
        factor_of = factor_of * one(*cut)
    return factor_of


def scatter_about(key, extent, scale, limit, cuts=(), held_as=jnp.bfloat16):
    result = scale * jax.random.normal(key, extent, jnp.float32)
    if cuts:
        result = result * shard_levels(key, extent, cuts, -0.22, 0.18)
    return jnp.clip(result, -limit, limit).astype(held_as)


def setup_inputs(seed: int = 0) -> dict:
    key_of = jax.random.split(jax.random.key(seed), 9)
    layer_input = draw_layer_input(jax.random.fold_in(key_of[8], 71), 0)
    norm_gain = jnp.clip(1.0 + 0.18 * jax.random.normal(key_of[1], (N_REPLICA, D), jnp.float32), 0.099609375, 1.8984375).astype(jnp.bfloat16)
    kv_weight = scatter_about(key_of[2], (N_REPLICA, D, 2 * KVW), D ** -0.5, 0.09375, ((0, 4), (1, 32)))
    kv_cotangent = scatter_about(key_of[3], (N_REPLICA, TOKENS, 2 * KVW), 1.0, 6.0, ((0, 4), (1, 32)))
    pseudo_grad = scatter_about(key_of[4], (N_REPLICA, FROWS, FCOLS), 1.0, 6.0, ((0, 4), (1, 32)), jnp.float32)
    outer_momentum = scatter_about(key_of[5], (FROWS, FCOLS), 0.5, 6.0, ((0, 32),), jnp.float32)
    global_params = scatter_about(key_of[6], (FROWS, FCOLS), 1.0, 6.0, ((0, 32),), jnp.float32)
    local_params = scatter_about(key_of[7], (N_REPLICA, FROWS, FCOLS), 1.0, 6.0, ((0, 4), (1, 32)))
    return dict(layer_input=layer_input, norm_gain=norm_gain, kv_weight=kv_weight, kv_cotangent=kv_cotangent, pseudo_grad=pseudo_grad, outer_momentum=outer_momentum, global_params=global_params, local_params=local_params)


epsilon = 1e-05
rope_base = 500000.0
momentum_rate = 0.9
outer_rate = 0.7
mixing_rate = 0.5

def angles_for(positions, head):
    half = head // 2
    index_f = jnp.arange(half, dtype=jnp.float32)
    inverse = jnp.exp(index_f * (-2.0 * math.log(rope_base) / head))
    angle = positions.astype(jnp.float32)[:, None] * inverse[None, :]
    return (jnp.cos(angle), jnp.sin(angle))

def rotate_keys(keys, cosine, sine, head, sign):
    count = keys.shape[0]
    shaped = keys.reshape(count, -1, head)
    half = head // 2
    first = shaped[:, :, :half]
    second = shaped[:, :, half:]
    cos_b = cosine[:, None, :]
    sin_b = sine[:, None, :] * sign
    out = jnp.concatenate([first * cos_b - second * sin_b, second * cos_b + first * sin_b], axis=2)
    return out.reshape(count, -1)

def inner_step(layer_input, norm_gain, kv_weight, kv_cotangent):
    tokens = layer_input.shape[0]
    kvw = kv_weight.shape[1] // 2
    positions = jnp.arange(tokens, dtype=jnp.int32) % SEQ_LEN
    cosine, sine = angles_for(positions, HEAD)
    values = layer_input.astype(jnp.float32)
    inv_rms = lax.rsqrt(lax.optimization_barrier(jnp.mean(values * values, axis=-1, keepdims=True)) + epsilon)
    normed = values * inv_rms
    gain_f = norm_gain.astype(jnp.float32)
    hidden = (normed * gain_f).astype(jnp.bfloat16)
    key_pre = jnp.dot(hidden, kv_weight, preferred_element_type=jnp.float32)
    kv_out = jnp.concatenate([rotate_keys(key_pre[:, :kvw], cosine, sine, HEAD, 1.0), key_pre[:, kvw:]], axis=1).astype(jnp.bfloat16)
    key_back = rotate_keys(kv_cotangent[:, :kvw].astype(jnp.float32), cosine, sine, HEAD, -1.0).astype(jnp.bfloat16)
    kv_grad = jnp.concatenate([key_back, kv_cotangent[:, kvw:]], axis=1)
    hidden_grad = lax.dot_general(kv_grad, kv_weight, (((1,), (1,)), ((), ())), preferred_element_type=jnp.float32)
    scale = 1.0 / math.sqrt(tokens)
    hidden_blocks = hidden.reshape(N_FSDP, TOK_DEV, D)
    grad_blocks = kv_grad.reshape(N_FSDP, TOK_DEV, 2 * kvw)
    prod_blocks = (hidden_grad * normed).reshape(N_FSDP, TOK_DEV, D)

    def add_block(carry, block):
        weight_sum, gain_sum = carry
        hidden_part, grad_part, prod_part = block
        weight_term = lax.dot_general(hidden_part, grad_part, (((0,), (0,)), ((), ())), preferred_element_type=jnp.float32) * scale
        gain_term = lax.optimization_barrier(jnp.sum(prod_part, axis=0)) * scale
        return ((weight_sum + weight_term, gain_sum + gain_term), None)
    start = (jnp.zeros((D, 2 * kvw), jnp.float32), jnp.zeros((D,), jnp.float32))
    (weight_grad, gain_grad), unused = lax.scan(add_block, start, (hidden_blocks, grad_blocks, prod_blocks))
    normed_grad = hidden_grad * gain_f
    input_grad = (inv_rms * (normed_grad - normed * lax.optimization_barrier(jnp.mean(normed_grad * normed, axis=-1, keepdims=True)))).astype(jnp.bfloat16)
    return (kv_out, input_grad, weight_grad, gain_grad)

def reference(layer_input, norm_gain, kv_weight, kv_cotangent, pseudo_grad, outer_momentum, global_params, local_params):
    kv_out, input_grad, weight_grad, gain_grad = lax.map(lambda group: inner_step(*group), (layer_input, norm_gain, kv_weight, kv_cotangent))
    average = lax.optimization_barrier(jnp.sum(pseudo_grad, axis=0)) / N_REPLICA
    momentum_new = momentum_rate * outer_momentum + average
    global_new = global_params - outer_rate * (average + momentum_rate * momentum_new)
    local_new = (mixing_rate * local_params.astype(jnp.float32) + (1.0 - mixing_rate) * global_new[None]).astype(jnp.bfloat16)
    return (kv_out, input_grad, weight_grad, gain_grad, momentum_new, global_new, local_new)
```

```python
import math

import jax
import jax.numpy as jnp
from jax import lax
from jax.experimental import pallas as pl
from jax.experimental.pallas import tpu as pltpu
from jax.sharding import PartitionSpec as P

HEAD = 128
SEQ_LEN = 4096
D = 4096
KV = 1024
TOK = 512
ROWS = 128
PARTS = 2
PSR = 384

epsilon = 1e-05
rope_base = 500000.0
momentum_rate = 0.9
outer_rate = 0.7
mixing_rate = 0.5

MESH = pl.DeviceIdType.MESH
BF = jnp.bfloat16
F32 = jnp.float32

SCATTER_ORDER = ((1, 2), (1, 1), (1, 3), (1, 0), (0, 2), (0, 1), (0, 3), (0, 0))
PER_PART = 41


def key_y(p):
    return p * PER_PART


def key_1(p, yr, step, way):
    return p * PER_PART + 1 + yr * 4 + step * 2 + way


def key_2(p, g, step, way):
    return p * PER_PART + 9 + (g[0] * 4 + g[1]) * 4 + step * 2 + way


def kernel(
    x_hbm,
    gain_hbm,
    w_hbm,
    ct_hbm,
    ps_hbm,
    om_hbm,
    gp_hbm,
    lp_hbm,
    cos_hbm,
    sin_hbm,
    kv_out,
    ig_out,
    wg_out,
    gg_out,
    mom_out,
    glob_out,
    loc_out,
    x_v,
    hid,
    wbuf,
    kv,
    kvt,
    pt,
    x1,
    x2,
    ybuf,
    gbuf,
    grow,
    invb,
    cb,
    pre,
    cos_v,
    sin_v,
    ps,
    psr,
    psum,
    srecv,
    trecv,
    om,
    gp,
    lp,
    lsem,
    ag_s,
    ag_r,
    rs_s,
    rs_r,
    g_s,
    g_r,
    p_s,
    p_r,
):
    rep = lax.axis_index("replica")
    me = lax.axis_index("fsdp")
    y = me // 16
    zc = (me // 4) % 4
    xc = me % 4
    core = rep % 2

    def at(yr, zo, xo):
        yy = y if yr == 0 else 1 - y
        zz = zc if zo == 0 else (zc + zo) % 4
        xx = xc if xo == 0 else (xc + xo) % 4
        return yy * 16 + zz * 4 + xx

    def shard(p, yr, o1, o2):
        return at(yr, o1, o2) if p == 0 else at(yr, o2, o1)

    shards = {
        (p, yr, o1, o2): shard(p, yr, o1, o2)
        for p in range(PARTS)
        for yr in range(2)
        for o1 in range(4)
        for o2 in range(4)
    }
    ypeer = at(1, 0, 0)
    peers1 = {(p, way): shards[p, 0, 1 if way == 0 else 3, 0] for p in range(PARTS) for way in range(2)}
    peers2 = {(p, way): shards[p, 0, 0, 1 if way == 0 else 3] for p in range(PARTS) for way in range(2)}
    gpeers = [at(0, 0, 1), at(0, 0, 2), at(0, 0, 3), at(0, 1, 0), at(0, 2, 0), at(0, 3, 0), ypeer]
    twin = rep + 1 - 2 * core
    across = (rep + 2) % 4
    half = 192
    mine = pl.multiple_of(core * half, half)
    other = pl.multiple_of((1 - core) * half, half)

    loads = {}

    def load(name, src, dst, k):
        loads[name] = pltpu.make_async_copy(src, dst, lsem.at[k])
        loads[name].start()

    own_rows = pl.multiple_of(me * ROWS, ROWS)
    load("w", w_hbm, wbuf.at[pl.ds(own_rows, ROWS)], 0)
    load("gain", gain_hbm, gbuf.at[me], 1)
    load("ps", ps_hbm, ps, 2)
    load("ct", ct_hbm, kv, 3)
    load("cos", cos_hbm, cos_v, 4)
    load("sin", sin_hbm, sin_v, 5)
    load("x", x_hbm, x_v, 6)
    load("om", om_hbm, om, 7)
    load("gp", gp_hbm, gp, 8)
    load("lp", lp_hbm, lp, 9)

    barrier = pltpu.get_barrier_semaphore()
    greet = [(rep, d) for d in gpeers] + [(twin, me), (across, me)]
    for dev in greet:
        pl.semaphore_signal(barrier, inc=1, device_id=dev, device_id_type=MESH)
    pl.semaphore_wait(barrier, len(greet))

    sent = []

    def remote(src, dst, ss, rs, dev):
        return pltpu.make_async_remote_copy(
            src_ref=src, dst_ref=dst, send_sem=ss, recv_sem=rs, device_id=dev, device_id_type=MESH
        )

    def wrows(p, s, piece):
        if piece is None:
            return wbuf.at[pl.ds(pl.multiple_of(s * ROWS + p * 64, 64), 64)]
        return wbuf.at[pl.ds(pl.multiple_of(s * ROWS + p * 64 + piece * 32, 32), 32)]

    def ag_send(p, s, piece, k, dev):
        ref = wrows(p, s, piece)
        remote(ref, ref, ag_s.at[k], ag_r.at[k], (rep, dev)).start()

    def ag_wait(p, s, piece, k):
        ref = wrows(p, s, piece)
        remote(ref, ref, ag_s.at[k], ag_r.at[k], (rep, ypeer)).wait_recv()

    def ag_y_send():
        for p in range(PARTS):
            ag_send(p, me, None, key_y(p), ypeer)

    def ag_y_wait():
        for p in range(PARTS):
            ag_wait(p, ypeer, None, key_y(p))

    def ag1_first(yr):
        for p in range(PARTS):
            for way in range(2):
                ag_send(p, shards[p, yr, 0, 0], None, key_1(p, yr, 0, way), peers1[p, way])

    def ag1_next(yr):
        for p in range(PARTS):
            for way in range(2):
                s = shards[p, yr, 3 if way == 0 else 1, 0]
                ag_wait(p, s, None, key_1(p, yr, 0, way))
                ag_send(p, s, way, key_1(p, yr, 1, way), peers1[p, way])

    def ag1_wait(yr):
        for p in range(PARTS):
            for way in range(2):
                ag_wait(p, shards[p, yr, 2, 0], way, key_1(p, yr, 1, way))

    def ag2_first(g):
        for p in range(PARTS):
            for way in range(2):
                ag_send(p, shards[p, g[0], g[1], 0], None, key_2(p, g, 0, way), peers2[p, way])

    def ag2_next(g):
        for p in range(PARTS):
            for way in range(2):
                s = shards[p, g[0], g[1], 3 if way == 0 else 1]
                ag_wait(p, s, None, key_2(p, g, 0, way))
                ag_send(p, s, way, key_2(p, g, 1, way), peers2[p, way])

    def ag2_wait(g):
        for p in range(PARTS):
            for way in range(2):
                ag_wait(p, shards[p, g[0], g[1], 2], way, key_2(p, g, 1, way))

    def prow(p, s, h, n):
        return pl.ds(pl.multiple_of(s * KV + p * 512 + h * 256, 256), n)

    def slot(p, stage, g, way):
        k = (g[0] * 4 + g[1]) if stage == 1 else 8 + g
        return (p * 10 + k) * 2 + way

    def rs_key(p, stage, g, step, way):
        return key_2(p, g, step, way) if stage == 1 else key_1(p, g, step, way)

    def rs_shard(p, stage, g, o):
        return shards[p, g[0], g[1], o] if stage == 1 else shards[p, g, o, 0]

    def rs_peer(p, stage, way):
        return peers2[p, way] if stage == 1 else peers1[p, way]

    def rs_first(stage, g):
        for p in range(PARTS):
            for way in range(2):
                k = rs_key(p, stage, g, 0, way)
                s = slot(p, stage, g, way)
                remote(
                    pt.at[prow(p, rs_shard(p, stage, g, 2), way, 256)],
                    x1.at[pl.ds(s * 256, 256)],
                    rs_s.at[k],
                    rs_r.at[k],
                    (rep, rs_peer(p, stage, way)),
                ).start()

    def rs_next(stage, g):
        for p in range(PARTS):
            for way in range(2):
                k = rs_key(p, stage, g, 0, way)
                s = slot(p, stage, g, way)
                ref = x1.at[pl.ds(s * 256, 256)]
                remote(ref, ref, rs_s.at[k], rs_r.at[k], (rep, ypeer)).wait_recv()
                to = rs_shard(p, stage, g, 1 if way == 0 else 3)
                r = prow(p, to, way, 256)
                pt[r, :] = (pt[r, :].astype(F32) + x1[pl.ds(s * 256, 256), :].astype(F32)).astype(BF)
                k = rs_key(p, stage, g, 1, way)
                remote(
                    pt.at[prow(p, to, 0, 512)],
                    x2.at[pl.ds(s * 512, 512)],
                    rs_s.at[k],
                    rs_r.at[k],
                    (rep, rs_peer(p, stage, way)),
                ).start()

    def rs_last(stage, g):
        for p in range(PARTS):
            for way in range(2):
                k = rs_key(p, stage, g, 1, way)
                ref = x2.at[pl.ds(slot(p, stage, g, way) * 512, 512)]
                remote(ref, ref, rs_s.at[k], rs_r.at[k], (rep, ypeer)).wait_recv()
            r = prow(p, rs_shard(p, stage, g, 0), 0, 512)
            a = x2[pl.ds(slot(p, stage, g, 0) * 512, 512), :].astype(F32)
            b = x2[pl.ds(slot(p, stage, g, 1) * 512, 512), :].astype(F32)
            pt[r, :] = (pt[r, :].astype(F32) + (a + b)).astype(BF)

    def rs_y_send():
        for p in range(PARTS):
            k = key_y(p)
            remote(
                pt.at[prow(p, ypeer, 0, 512)],
                ybuf.at[pl.ds(p * 512, 512)],
                rs_s.at[k],
                rs_r.at[k],
                (rep, ypeer),
            ).start()

    def rs_y_wait():
        for p in range(PARTS):
            k = key_y(p)
            ref = ybuf.at[pl.ds(p * 512, 512)]
            remote(ref, ref, rs_s.at[k], rs_r.at[k], (rep, ypeer)).wait_recv()

    def gain_ref(stage, yr, off):
        if stage == 0:
            return gbuf.at[at(yr, 0, off)]
        if stage == 1:
            return gbuf.at[pl.ds(at(yr, off, 0) // 4 * 4, 4)]
        return gbuf.at[pl.ds(at(yr, 0, 0) // 16 * 16, 16)]

    def gain_send(stage):
        for o in (1, 2, 3) if stage < 2 else (0,):
            k = stage * 3 + max(o, 1) - 1
            ref = gain_ref(stage, 0, 0)
            remote(ref, ref, g_s.at[k], g_r.at[k], (rep, gpeers[k])).start()

    def gain_wait(stage):
        for o in (1, 2, 3) if stage < 2 else (0,):
            k = stage * 3 + max(o, 1) - 1
            ref = gain_ref(stage, 0, 4 - o) if stage < 2 else gain_ref(2, 1, 0)
            remote(ref, ref, g_s.at[k], g_r.at[k], (rep, ypeer)).wait_recv()

    def ps_send(k):
        if k == 0:
            src, dst, dev = ps.at[pl.ds(other, half)], psr, (twin, me)
        elif k == 1:
            src, dst, dev = psum, srecv, (across, me)
        else:
            src, dst, dev = ps.at[pl.ds(mine, half)], trecv, (twin, me)
        remote(src, dst, p_s.at[k], p_r.at[k], dev).start()

    def ps_wait(k):
        ref = (psr, srecv, trecv)[k]
        remote(ref, ref, p_s.at[k], p_r.at[k], (twin, me)).wait_recv()

    def ps_sent(k):
        ref = (psr, srecv, trecv)[k]
        remote(ref, ref, p_s.at[k], p_r.at[k], (twin, me)).wait_send()

    loads["w"].wait()
    ag1_first(0)
    ag_y_send()
    ag2_first((0, 0))
    loads["gain"].wait()
    gain_send(0)
    loads["ps"].wait()
    ps_send(0)

    loads["ct"].wait()
    loads["cos"].wait()
    loads["sin"].wait()

    @pl.loop(0, 4)
    def _(h):
        cols = pl.ds(pl.multiple_of(h * HEAD, HEAD), HEAD)
        v = kv[:, cols].astype(F32)
        r = (v * cos_v[...] - pltpu.roll(v, HEAD // 2, 1) * sin_v[...]).astype(BF)
        kv[:, cols] = r
        kvt[cols, :] = r.T

    @pl.loop(4, 8)
    def _(h):
        cols = pl.ds(pl.multiple_of(h * HEAD, HEAD), HEAD)
        kvt[cols, :] = kv[:, cols].T

    gain_wait(0)
    gain_send(1)
    ag1_next(0)

    ps_wait(0)
    ps_sent(0)

    @pl.loop(0, 12)
    def _(i):
        r = pl.ds(pl.multiple_of(i * 16, 16), 16)
        rm = pl.ds(pl.multiple_of(mine + i * 16, 16), 16)
        psum[r, :] = ps[rm, :] + psr[r, :]

    ps_send(1)
    gain_wait(1)
    gain_send(2)

    ag_y_wait()
    ag1_first(1)
    ag2_first((0, 3))
    ag2_first((0, 1))

    gain_wait(2)
    for j in range(32):
        grow[:, j * 128 : (j + 1) * 128] = jnp.broadcast_to(gbuf[j], (8, 128))
    loads["x"].wait()

    @pl.loop(0, TOK // 16)
    def _(i):
        r = pl.ds(pl.multiple_of(i * 16, 16), 16)
        v = x_v[r, :].astype(F32)
        inv = lax.rsqrt(jnp.mean(v * v, axis=-1, keepdims=True) + epsilon)
        invb[r, :] = jnp.broadcast_to(inv, (16, 128))
        hid[r, :] = (x_v[r, :].astype(F32) * inv * grow[0:1, :]).astype(BF)

    def ag_a():
        ag2_next((0, 0))
        ag2_first((1, 0))

    def ag_b():
        ag1_next(1)

    def ag_c():
        ag2_next((0, 3))
        ag1_wait(0)
        ag2_first((0, 2))

    def ag_d():
        ag2_next((0, 1))
        ag2_first((1, 3))

    def ag_e():
        ag2_next((1, 0))
        ag2_first((1, 1))

    steps = {0: ag_a, 3: ag_b, 6: ag_c, 9: ag_d, 12: ag_e}

    @pl.loop(0, 16)
    def _(i):
        for k, fn in steps.items():
            pl.when(i == k)(fn)
        res = jnp.dot(
            kvt[...],
            hid[:, pl.ds(pl.multiple_of(i * 256, 256), 256)],
            preferred_element_type=F32,
        )
        r0 = pl.multiple_of(i * 2048, 2048)
        pt[pl.ds(r0, 1024), :] = res[:, :128].astype(BF)
        pt[pl.ds(r0 + 1024, 1024), :] = res[:, 128:].astype(BF)

    ag1_wait(1)
    ag2_first((1, 2))
    ag2_next((0, 2))

    ps_wait(1)
    ps_sent(1)

    @pl.loop(0, 12)
    def _(i):
        r = pl.ds(pl.multiple_of(i * 16, 16), 16)
        rm = pl.ds(pl.multiple_of(mine + i * 16, 16), 16)
        ps[rm, :] = psum[r, :] + srecv[r, :]

    ps_send(2)
    ag2_next((1, 3))
    ag2_next((1, 1))
    ps_wait(2)
    ps_sent(2)
    loads["om"].wait()
    loads["gp"].wait()
    loads["lp"].wait()

    def update(r, total):
        average = total * 0.25
        m = momentum_rate * om[r, :] + average
        gn = gp[r, :] - outer_rate * (average + momentum_rate * m)
        mom_out[r, :] = m
        glob_out[r, :] = gn
        loc_out[r, :] = (mixing_rate * lp[r, :].astype(F32) + (1.0 - mixing_rate) * gn).astype(BF)

    @pl.loop(0, 12)
    def _(i):
        rm = pl.ds(pl.multiple_of(mine + i * 16, 16), 16)
        update(rm, ps[rm, :])
        ro = pl.ds(pl.multiple_of(other + i * 16, 16), 16)
        update(ro, trecv[pl.ds(pl.multiple_of(i * 16, 16), 16), :])

    ag2_next((1, 2))
    order = SCATTER_ORDER
    rs_first(1, order[0])
    rs_first(1, order[1])
    for yr in range(2):
        for o in range(4):
            ag2_wait((yr, o))

    def r0():
        rs_first(1, order[2])
        rs_next(1, order[0])

    def r1():
        rs_first(1, order[3])
        rs_next(1, order[1])

    def r2():
        rs_first(1, order[4])
        rs_next(1, order[2])

    def r2b():
        rs_last(1, order[0])
        rs_first(2, 1)

    def r3():
        rs_first(1, order[5])
        rs_next(1, order[3])
        rs_last(1, order[1])

    def r4():
        rs_first(1, order[6])
        rs_next(1, order[4])

    def r4b():
        rs_last(1, order[2])
        rs_next(2, 1)

    def r5():
        rs_first(1, order[7])
        rs_next(1, order[5])
        rs_last(1, order[3])

    def r6():
        rs_next(1, order[6])
        rs_last(1, order[4])
        rs_first(2, 0)

    def r6b():
        rs_last(2, 1)
        rs_y_send()

    def r7():
        rs_next(1, order[7])
        rs_last(1, order[5])

    def r8():
        rs_last(1, order[6])
        rs_next(2, 0)

    def r9():
        rs_last(1, order[7])

    cb[...] = jnp.zeros_like(cb)
    fwd_steps = {0: r0, 1: r1, 2: r2, 3: r2b}

    @pl.loop(0, 4)
    def _(n):
        for k, fn in fwd_steps.items():
            pl.when(n == k)(fn)
        cols = pl.ds(pl.multiple_of(n * 256, 256), 256)
        pre[...] = jnp.dot(hid[...], wbuf[:, cols], preferred_element_type=F32)
        for b in range(2):
            c128 = pl.ds(pl.multiple_of(n * 256 + b * 128, 128), 128)
            v = pre[:, b * 128 : (b + 1) * 128]
            cb[...] += v * kv[:, c128].astype(F32)

            @pl.when(n < 2)
            def _():
                v = pre[:, b * 128 : (b + 1) * 128]
                kv_out[:, c128] = (v * cos_v[...] + pltpu.roll(v, HEAD // 2, 1) * sin_v[...]).astype(BF)

            @pl.when(n >= 2)
            def _():
                kv_out[:, c128] = pre[:, b * 128 : (b + 1) * 128].astype(BF)

    cb[...] = jnp.broadcast_to(jnp.sum(cb[...], axis=-1, keepdims=True) * (1.0 / D), (TOK, 128))

    bwd_steps = {0: r3, 2: r4, 4: r4b, 5: r5, 8: r6, 10: r6b, 12: r7, 15: r8}

    @pl.loop(0, 16)
    def _(i):
        for k, fn in bwd_steps.items():
            pl.when(i == k)(fn)
        rows = pl.ds(pl.multiple_of(i * 256, 256), 256)
        pre[...] = lax.dot_general(
            kv[...], wbuf[rows, :], (((1,), (1,)), ((), ())), preferred_element_type=F32
        )
        for b in range(2):
            cols = pl.ds(pl.multiple_of(i * 256 + b * 128, 128), 128)
            inv = invb[...]
            normed = x_v[:, cols].astype(F32) * inv
            ng = pre[:, b * 128 : (b + 1) * 128] * grow[0:1, cols]
            ig_out[:, cols] = (inv * (ng - normed * cb[...])).astype(BF)

    r9()
    rs_last(2, 0)
    rs_y_wait()
    scale = 1.0 / math.sqrt(TOK * 32)
    acc = jnp.zeros((128, 128), F32)
    for k in range(8):
        r = pl.ds(pl.multiple_of(me * KV + k * 128, 128), 128)
        t = ((pt[r, :].astype(F32) + ybuf[k * 128 : (k + 1) * 128, :].astype(F32)) * scale).T
        wg_out[:, k * 128 : (k + 1) * 128] = t
        acc = acc + t * wbuf[pl.ds(own_rows, ROWS), k * 128 : (k + 1) * 128].astype(F32)
    gg_out[...] = jnp.sum(acc.T, axis=0, keepdims=True) / gbuf[me]

    def done(ref, sem):
        remote(ref, ref, sem, g_r.at[0], (rep, ypeer)).wait_send()

    for p in range(PARTS):
        done(wbuf.at[pl.ds(0, 64)], ag_s.at[key_y(p)])
        done(ybuf.at[pl.ds(0, 512)], rs_s.at[key_y(p)])
        for step in range(2):
            for way in range(2):
                keys = [key_1(p, yr, step, way) for yr in range(2)]
                keys += [key_2(p, (yr, o), step, way) for yr in range(2) for o in range(4)]
                for k in keys:
                    done(wbuf.at[pl.ds(0, 32 if step else 64)], ag_s.at[k])
                    done(ybuf.at[pl.ds(0, 512 if step else 256)], rs_s.at[k])
    for k in range(7):
        done(gain_ref(k // 3, 0, 0), g_s.at[k])


def local(
    layer_input,
    norm_gain,
    kv_weight,
    kv_cotangent,
    pseudo_grad,
    outer_momentum,
    global_params,
    local_params,
):
    positions = (lax.axis_index("fsdp") * TOK + jnp.arange(TOK, dtype=jnp.int32)) % SEQ_LEN
    lane = jnp.arange(HEAD, dtype=jnp.int32)
    index_f = (lane % (HEAD // 2)).astype(F32)
    inverse = jnp.exp(index_f * (-2.0 * math.log(rope_base) / HEAD))
    angle = positions.astype(F32)[:, None] * inverse[None, :]
    cosine = jnp.cos(angle)
    sine = jnp.sin(angle) * jnp.where(lane < HEAD // 2, -1.0, 1.0)[None, :]
    any_spec = pl.BlockSpec(memory_space=pl.ANY)
    vmem = pl.BlockSpec(memory_space=pltpu.VMEM)
    dma = pltpu.SemaphoreType.DMA
    outs = pl.pallas_call(
        kernel,
        out_shape=(
            jax.ShapeDtypeStruct((TOK, KV), BF),
            jax.ShapeDtypeStruct((TOK, D), BF),
            jax.ShapeDtypeStruct((ROWS, KV), F32),
            jax.ShapeDtypeStruct((1, ROWS), F32),
            jax.ShapeDtypeStruct((PSR, KV), F32),
            jax.ShapeDtypeStruct((PSR, KV), F32),
            jax.ShapeDtypeStruct((PSR, KV), BF),
        ),
        in_specs=[any_spec] * 10,
        out_specs=(vmem,) * 7,
        scratch_shapes=[
            pltpu.VMEM((TOK, D), BF),
            pltpu.VMEM((TOK, D), BF),
            pltpu.VMEM((D, KV), BF),
            pltpu.VMEM((TOK, KV), BF),
            pltpu.VMEM((KV, TOK), BF),
            pltpu.VMEM((32 * KV, ROWS), BF),
            pltpu.VMEM((40 * 256, ROWS), BF),
            pltpu.VMEM((40 * 512, ROWS), BF),
            pltpu.VMEM((KV, ROWS), BF),
            pltpu.VMEM((32, 1, ROWS), F32),
            pltpu.VMEM((8, D), F32),
            pltpu.VMEM((TOK, 128), F32),
            pltpu.VMEM((TOK, 128), F32),
            pltpu.VMEM((TOK, 256), F32),
            pltpu.VMEM((TOK, 128), F32),
            pltpu.VMEM((TOK, 128), F32),
            pltpu.VMEM((PSR, KV), F32),
            pltpu.VMEM((PSR // 2, KV), F32),
            pltpu.VMEM((PSR // 2, KV), F32),
            pltpu.VMEM((PSR // 2, KV), F32),
            pltpu.VMEM((PSR // 2, KV), F32),
            pltpu.VMEM((PSR, KV), F32),
            pltpu.VMEM((PSR, KV), F32),
            pltpu.VMEM((PSR, KV), BF),
            dma((10,)),
            dma((2 * PER_PART,)),
            dma((2 * PER_PART,)),
            dma((2 * PER_PART,)),
            dma((2 * PER_PART,)),
            dma((7,)),
            dma((7,)),
            dma((3,)),
            dma((3,)),
        ],
        compiler_params=pltpu.CompilerParams(
            collective_id=0, has_side_effects=True, vmem_limit_bytes=63 * 1024 * 1024
        ),
    )(
        layer_input[0],
        norm_gain.astype(F32),
        kv_weight[0],
        kv_cotangent[0],
        pseudo_grad[0],
        outer_momentum,
        global_params,
        local_params[0],
        cosine,
        sine,
    )
    kv_out, input_grad, weight_grad, gain_grad, momentum_new, global_new, local_new = outs
    return (
        kv_out[None],
        input_grad[None],
        weight_grad[None],
        gain_grad,
        momentum_new,
        global_new,
        local_new[None],
    )


def solution(mesh):
    shared = P("replica", "fsdp", None)
    in_specs = (
        shared,
        P("replica", "fsdp"),
        shared,
        shared,
        shared,
        P("fsdp", None),
        P("fsdp", None),
        shared,
    )
    out_specs = (
        shared,
        shared,
        shared,
        P("replica", "fsdp"),
        P("fsdp", None),
        P("fsdp", None),
        shared,
    )
    return jax.shard_map(local, mesh=mesh, in_specs=in_specs, out_specs=out_specs, check_vma=False)
```

```python
import math

import jax
import jax.numpy as jnp
from jax import lax
from jax.experimental import pallas as pl
from jax.experimental.pallas import tpu as pltpu
from jax.sharding import PartitionSpec as P

HEAD = 128
SEQ_LEN = 4096
D = 4096
KV = 1024
TOK = 512
ROWS = 128
PARTS = 2
PSR = 384

epsilon = 1e-05
rope_base = 500000.0
momentum_rate = 0.9
outer_rate = 0.7
mixing_rate = 0.5

TURN_MID = 507 / 262144
TURN_LOW = 2 * math.pi - 6.28125 - TURN_MID

MESH = pl.DeviceIdType.MESH
BF = jnp.bfloat16
F32 = jnp.float32

SCATTER_ORDER = ((1, 2), (1, 1), (1, 3), (1, 0), (0, 2), (0, 1), (0, 3), (0, 0))
PER_PART = 41


def key_y(p):
    return p * PER_PART


def key_1(p, yr, step, way):
    return p * PER_PART + 1 + yr * 4 + step * 2 + way


def key_2(p, g, step, way):
    return p * PER_PART + 9 + (g[0] * 4 + g[1]) * 4 + step * 2 + way


def kernel(
    x_hbm,
    gain_v,
    w_hbm,
    ct_hbm,
    ps_hbm,
    om_hbm,
    gp_hbm,
    lp_hbm,
    kv_out,
    ig_out,
    wg_out,
    gg_out,
    mom_out,
    glob_out,
    loc_out,
    x_v,
    hid,
    wbuf,
    kv,
    kvt,
    pt,
    x1,
    x2,
    ybuf,
    gbuf,
    grow,
    invb,
    cb,
    pre,
    cos_v,
    sin_v,
    ps,
    psr,
    psum,
    srecv,
    trecv,
    om,
    gp,
    lp,
    lsem,
    ag_s,
    ag_r,
    rs_s,
    rs_r,
    g_s,
    g_r,
    p_s,
    p_r,
):
    rep = lax.axis_index("replica")
    me = lax.axis_index("fsdp")
    y = me // 16
    zc = (me // 4) % 4
    xc = me % 4
    core = rep % 2

    def at(yr, zo, xo):
        yy = y if yr == 0 else 1 - y
        zz = zc if zo == 0 else (zc + zo) % 4
        xx = xc if xo == 0 else (xc + xo) % 4
        return yy * 16 + zz * 4 + xx

    def shard(p, yr, o1, o2):
        return at(yr, o1, o2) if p == 0 else at(yr, o2, o1)

    shards = {
        (p, yr, o1, o2): shard(p, yr, o1, o2)
        for p in range(PARTS)
        for yr in range(2)
        for o1 in range(4)
        for o2 in range(4)
    }
    ypeer = at(1, 0, 0)
    peers1 = {(p, way): shards[p, 0, 1 if way == 0 else 3, 0] for p in range(PARTS) for way in range(2)}
    peers2 = {(p, way): shards[p, 0, 0, 1 if way == 0 else 3] for p in range(PARTS) for way in range(2)}
    gpeers = [at(0, 0, 1), at(0, 0, 2), at(0, 0, 3), at(0, 1, 0), at(0, 2, 0), at(0, 3, 0), ypeer]
    twin = rep + 1 - 2 * core
    across = (rep + 2) % 4
    half = 192
    mine = pl.multiple_of(core * half, half)
    other = pl.multiple_of((1 - core) * half, half)

    loads = {}

    def load(name, src, dst, k):
        loads[name] = pltpu.make_async_copy(src, dst, lsem.at[k])
        loads[name].start()

    own_rows = pl.multiple_of(me * ROWS, ROWS)
    load("w", w_hbm, wbuf.at[pl.ds(own_rows, ROWS)], 0)
    load("ps", ps_hbm, ps, 2)
    load("ct", ct_hbm, kv, 3)
    load("x", x_hbm, x_v, 6)
    load("om", om_hbm, om, 7)
    load("gp", gp_hbm, gp, 8)
    load("lp", lp_hbm, lp, 9)

    gbuf[me] = gain_v[...].astype(F32)
    barrier = pltpu.get_barrier_semaphore()
    greet = [(rep, d) for d in gpeers] + [(twin, me), (across, me)]
    for dev in greet:
        pl.semaphore_signal(barrier, inc=1, device_id=dev, device_id_type=MESH)
    pl.semaphore_wait(barrier, len(greet))

    sent = []

    def remote(src, dst, ss, rs, dev):
        return pltpu.make_async_remote_copy(
            src_ref=src, dst_ref=dst, send_sem=ss, recv_sem=rs, device_id=dev, device_id_type=MESH
        )

    def wrows(p, s, piece):
        if piece is None:
            return wbuf.at[pl.ds(pl.multiple_of(s * ROWS + p * 64, 64), 64)]
        return wbuf.at[pl.ds(pl.multiple_of(s * ROWS + p * 64 + piece * 32, 32), 32)]

    def ag_send(p, s, piece, k, dev):
        ref = wrows(p, s, piece)
        remote(ref, ref, ag_s.at[k], ag_r.at[k], (rep, dev)).start()

    def ag_wait(p, s, piece, k):
        ref = wrows(p, s, piece)
        remote(ref, ref, ag_s.at[k], ag_r.at[k], (rep, ypeer)).wait_recv()

    def ag_y_send():
        for p in range(PARTS):
            ag_send(p, me, None, key_y(p), ypeer)

    def ag_y_wait():
        for p in range(PARTS):
            ag_wait(p, ypeer, None, key_y(p))

    def ag1_first(yr):
        for p in range(PARTS):
            for way in range(2):
                ag_send(p, shards[p, yr, 0, 0], None, key_1(p, yr, 0, way), peers1[p, way])

    def ag1_next(yr):
        for p in range(PARTS):
            for way in range(2):
                s = shards[p, yr, 3 if way == 0 else 1, 0]
                ag_wait(p, s, None, key_1(p, yr, 0, way))
                ag_send(p, s, way, key_1(p, yr, 1, way), peers1[p, way])

    def ag1_wait(yr):
        for p in range(PARTS):
            for way in range(2):
                ag_wait(p, shards[p, yr, 2, 0], way, key_1(p, yr, 1, way))

    def ag2_first(g):
        for p in range(PARTS):
            for way in range(2):
                ag_send(p, shards[p, g[0], g[1], 0], None, key_2(p, g, 0, way), peers2[p, way])

    def ag2_next(g):
        for p in range(PARTS):
            for way in range(2):
                s = shards[p, g[0], g[1], 3 if way == 0 else 1]
                ag_wait(p, s, None, key_2(p, g, 0, way))
                ag_send(p, s, way, key_2(p, g, 1, way), peers2[p, way])

    def ag2_wait(g):
        for p in range(PARTS):
            for way in range(2):
                ag_wait(p, shards[p, g[0], g[1], 2], way, key_2(p, g, 1, way))

    def prow(p, s, h, n):
        return pl.ds(pl.multiple_of(s * KV + p * 512 + h * 256, 256), n)

    def slot(p, stage, g, way):
        k = (g[0] * 4 + g[1]) if stage == 1 else 8 + g
        return (p * 10 + k) * 2 + way

    def rs_key(p, stage, g, step, way):
        return key_2(p, g, step, way) if stage == 1 else key_1(p, g, step, way)

    def rs_shard(p, stage, g, o):
        return shards[p, g[0], g[1], o] if stage == 1 else shards[p, g, o, 0]

    def rs_peer(p, stage, way):
        return peers2[p, way] if stage == 1 else peers1[p, way]

    def rs_first(stage, g):
        for p in range(PARTS):
            for way in range(2):
                k = rs_key(p, stage, g, 0, way)
                s = slot(p, stage, g, way)
                remote(
                    pt.at[prow(p, rs_shard(p, stage, g, 2), way, 256)],
                    x1.at[pl.ds(s * 256, 256)],
                    rs_s.at[k],
                    rs_r.at[k],
                    (rep, rs_peer(p, stage, way)),
                ).start()

    def rs_next(stage, g):
        for p in range(PARTS):
            for way in range(2):
                k = rs_key(p, stage, g, 0, way)
                s = slot(p, stage, g, way)
                ref = x1.at[pl.ds(s * 256, 256)]
                remote(ref, ref, rs_s.at[k], rs_r.at[k], (rep, ypeer)).wait_recv()
                to = rs_shard(p, stage, g, 1 if way == 0 else 3)
                r = prow(p, to, way, 256)
                pt[r, :] = (pt[r, :].astype(F32) + x1[pl.ds(s * 256, 256), :].astype(F32)).astype(BF)
                k = rs_key(p, stage, g, 1, way)
                remote(
                    pt.at[prow(p, to, 0, 512)],
                    x2.at[pl.ds(s * 512, 512)],
                    rs_s.at[k],
                    rs_r.at[k],
                    (rep, rs_peer(p, stage, way)),
                ).start()

    def rs_last(stage, g):
        for p in range(PARTS):
            for way in range(2):
                k = rs_key(p, stage, g, 1, way)
                ref = x2.at[pl.ds(slot(p, stage, g, way) * 512, 512)]
                remote(ref, ref, rs_s.at[k], rs_r.at[k], (rep, ypeer)).wait_recv()
            r = prow(p, rs_shard(p, stage, g, 0), 0, 512)
            a = x2[pl.ds(slot(p, stage, g, 0) * 512, 512), :].astype(F32)
            b = x2[pl.ds(slot(p, stage, g, 1) * 512, 512), :].astype(F32)
            pt[r, :] = (pt[r, :].astype(F32) + (a + b)).astype(BF)

    def rs_y_send():
        for p in range(PARTS):
            k = key_y(p)
            remote(
                pt.at[prow(p, ypeer, 0, 512)],
                ybuf.at[pl.ds(p * 512, 512)],
                rs_s.at[k],
                rs_r.at[k],
                (rep, ypeer),
            ).start()

    def rs_y_wait():
        for p in range(PARTS):
            k = key_y(p)
            ref = ybuf.at[pl.ds(p * 512, 512)]
            remote(ref, ref, rs_s.at[k], rs_r.at[k], (rep, ypeer)).wait_recv()

    def gain_ref(stage, yr, off):
        if stage == 0:
            return gbuf.at[at(yr, 0, off)]
        if stage == 1:
            return gbuf.at[pl.ds(at(yr, off, 0) // 4 * 4, 4)]
        return gbuf.at[pl.ds(at(yr, 0, 0) // 16 * 16, 16)]

    def gain_send(stage):
        for o in (1, 2, 3) if stage < 2 else (0,):
            k = stage * 3 + max(o, 1) - 1
            ref = gain_ref(stage, 0, 0)
            remote(ref, ref, g_s.at[k], g_r.at[k], (rep, gpeers[k])).start()

    def gain_wait(stage):
        for o in (1, 2, 3) if stage < 2 else (0,):
            k = stage * 3 + max(o, 1) - 1
            ref = gain_ref(stage, 0, 4 - o) if stage < 2 else gain_ref(2, 1, 0)
            remote(ref, ref, g_s.at[k], g_r.at[k], (rep, ypeer)).wait_recv()

    def ps_send(k):
        if k == 0:
            src, dst, dev = ps.at[pl.ds(other, half)], psr, (twin, me)
        elif k == 1:
            src, dst, dev = psum, srecv, (across, me)
        else:
            src, dst, dev = ps.at[pl.ds(mine, half)], trecv, (twin, me)
        remote(src, dst, p_s.at[k], p_r.at[k], dev).start()

    def ps_wait(k):
        ref = (psr, srecv, trecv)[k]
        remote(ref, ref, p_s.at[k], p_r.at[k], (twin, me)).wait_recv()

    def ps_sent(k):
        ref = (psr, srecv, trecv)[k]
        remote(ref, ref, p_s.at[k], p_r.at[k], (twin, me)).wait_send()

    loads["w"].wait()
    ag1_first(0)
    ag_y_send()
    ag2_first((0, 0))
    loads["ps"].wait()
    ps_send(0)
    gain_send(0)

    lane = lax.broadcasted_iota(jnp.int32, (8, HEAD), 1)
    inverse = jnp.exp((lane % (HEAD // 2)).astype(F32) * (-2.0 * math.log(rope_base) / HEAD))
    sign = jnp.where(lane < HEAD // 2, -1.0, 1.0)
    first_position = (me * TOK) % SEQ_LEN

    @pl.loop(0, TOK // 8)
    def _(i):
        r = pl.ds(pl.multiple_of(i * 8, 8), 8)
        position = first_position + i * 8 + lax.broadcasted_iota(jnp.int32, (8, HEAD), 0)
        angle = position.astype(F32) * inverse
        turns = jnp.round(angle * (0.5 / math.pi))
        angle = ((angle - turns * 6.28125) - turns * TURN_MID) - turns * TURN_LOW
        cos_v[r, :] = jnp.cos(angle)
        sin_v[r, :] = jnp.sin(angle) * sign

    loads["ct"].wait()

    @pl.loop(0, 4)
    def _(h):
        cols = pl.ds(pl.multiple_of(h * HEAD, HEAD), HEAD)
        v = kv[:, cols].astype(F32)
        r = (v * cos_v[...] - pltpu.roll(v, HEAD // 2, 1) * sin_v[...]).astype(BF)
        kv[:, cols] = r
        kvt[cols, :] = r.T

    @pl.loop(4, 8)
    def _(h):
        cols = pl.ds(pl.multiple_of(h * HEAD, HEAD), HEAD)
        kvt[cols, :] = kv[:, cols].T

    gain_wait(0)
    gain_send(1)
    ag1_next(0)

    ps_wait(0)
    ps_sent(0)

    @pl.loop(0, 12)
    def _(i):
        r = pl.ds(pl.multiple_of(i * 16, 16), 16)
        rm = pl.ds(pl.multiple_of(mine + i * 16, 16), 16)
        psum[r, :] = ps[rm, :] + psr[r, :]

    ps_send(1)
    gain_wait(1)
    gain_send(2)

    ag_y_wait()
    ag1_first(1)
    ag2_first((0, 3))
    ag2_first((0, 1))

    gain_wait(2)
    for j in range(32):
        grow[:, j * 128 : (j + 1) * 128] = jnp.broadcast_to(gbuf[j], (8, 128))
    loads["x"].wait()

    @pl.loop(0, TOK // 16)
    def _(i):
        r = pl.ds(pl.multiple_of(i * 16, 16), 16)
        v = x_v[r, :].astype(F32)
        inv = lax.rsqrt(jnp.mean(v * v, axis=-1, keepdims=True) + epsilon)
        invb[r, :] = jnp.broadcast_to(inv, (16, 128))
        hid[r, :] = (x_v[r, :].astype(F32) * inv * grow[0:1, :]).astype(BF)

    def ag_a():
        ag2_next((0, 0))
        ag2_first((1, 0))

    def ag_b():
        ag1_next(1)

    def ag_c():
        ag2_next((0, 3))
        ag1_wait(0)
        ag2_first((0, 2))

    def ag_d():
        ag2_next((0, 1))
        ag2_first((1, 3))

    def ag_e():
        ag2_next((1, 0))
        ag2_first((1, 1))

    steps = {0: ag_a, 3: ag_b, 6: ag_c, 9: ag_d, 12: ag_e}

    @pl.loop(0, 16)
    def _(i):
        for k, fn in steps.items():
            pl.when(i == k)(fn)
        res = jnp.dot(
            kvt[...],
            hid[:, pl.ds(pl.multiple_of(i * 256, 256), 256)],
            preferred_element_type=F32,
        )
        r0 = pl.multiple_of(i * 2048, 2048)
        pt[pl.ds(r0, 1024), :] = res[:, :128].astype(BF)
        pt[pl.ds(r0 + 1024, 1024), :] = res[:, 128:].astype(BF)

    ag1_wait(1)
    ag2_first((1, 2))
    ag2_next((0, 2))

    ps_wait(1)
    ps_sent(1)

    @pl.loop(0, 12)
    def _(i):
        r = pl.ds(pl.multiple_of(i * 16, 16), 16)
        rm = pl.ds(pl.multiple_of(mine + i * 16, 16), 16)
        ps[rm, :] = psum[r, :] + srecv[r, :]

    ps_send(2)
    ag2_next((1, 3))
    ag2_next((1, 1))
    ps_wait(2)
    ps_sent(2)
    loads["om"].wait()
    loads["gp"].wait()
    loads["lp"].wait()

    def update(r, total):
        average = total * 0.25
        m = momentum_rate * om[r, :] + average
        gn = gp[r, :] - outer_rate * (average + momentum_rate * m)
        mom_out[r, :] = m
        glob_out[r, :] = gn
        loc_out[r, :] = (mixing_rate * lp[r, :].astype(F32) + (1.0 - mixing_rate) * gn).astype(BF)

    @pl.loop(0, 12)
    def _(i):
        rm = pl.ds(pl.multiple_of(mine + i * 16, 16), 16)
        update(rm, ps[rm, :])
        ro = pl.ds(pl.multiple_of(other + i * 16, 16), 16)
        update(ro, trecv[pl.ds(pl.multiple_of(i * 16, 16), 16), :])

    ag2_next((1, 2))
    order = SCATTER_ORDER
    rs_first(1, order[0])
    rs_first(1, order[1])
    for yr in range(2):
        for o in range(4):
            ag2_wait((yr, o))

    def r0():
        rs_first(1, order[2])
        rs_next(1, order[0])

    def r1():
        rs_first(1, order[3])
        rs_next(1, order[1])

    def r2():
        rs_first(1, order[4])
        rs_next(1, order[2])

    def r2b():
        rs_last(1, order[0])
        rs_first(2, 1)

    def r3():
        rs_first(1, order[5])
        rs_next(1, order[3])
        rs_last(1, order[1])

    def r4():
        rs_first(1, order[6])
        rs_next(1, order[4])

    def r4b():
        rs_last(1, order[2])
        rs_next(2, 1)

    def r5():
        rs_first(1, order[7])
        rs_next(1, order[5])
        rs_last(1, order[3])

    def r6():
        rs_next(1, order[6])
        rs_last(1, order[4])
        rs_first(2, 0)

    def r6b():
        rs_last(2, 1)
        rs_y_send()

    def r7():
        rs_next(1, order[7])
        rs_last(1, order[5])

    def r8():
        rs_last(1, order[6])
        rs_next(2, 0)

    def r9():
        rs_last(1, order[7])

    cb[...] = jnp.zeros_like(cb)
    fwd_steps = {0: r0, 1: r1, 2: r2, 3: r2b}

    @pl.loop(0, 4)
    def _(n):
        for k, fn in fwd_steps.items():
            pl.when(n == k)(fn)
        cols = pl.ds(pl.multiple_of(n * 256, 256), 256)
        pre[...] = jnp.dot(hid[...], wbuf[:, cols], preferred_element_type=F32)
        for b in range(2):
            c128 = pl.ds(pl.multiple_of(n * 256 + b * 128, 128), 128)
            v = pre[:, b * 128 : (b + 1) * 128]
            cb[...] += v * kv[:, c128].astype(F32)

            @pl.when(n < 2)
            def _():
                v = pre[:, b * 128 : (b + 1) * 128]
                kv_out[:, c128] = (v * cos_v[...] + pltpu.roll(v, HEAD // 2, 1) * sin_v[...]).astype(BF)

            @pl.when(n >= 2)
            def _():
                kv_out[:, c128] = pre[:, b * 128 : (b + 1) * 128].astype(BF)

    cb[...] = jnp.broadcast_to(jnp.sum(cb[...], axis=-1, keepdims=True) * (1.0 / D), (TOK, 128))

    bwd_steps = {0: r3, 2: r4, 4: r4b, 5: r5, 8: r6, 10: r6b, 12: r7, 15: r8}

    @pl.loop(0, 16)
    def _(i):
        for k, fn in bwd_steps.items():
            pl.when(i == k)(fn)
        rows = pl.ds(pl.multiple_of(i * 256, 256), 256)
        pre[...] = lax.dot_general(
            kv[...], wbuf[rows, :], (((1,), (1,)), ((), ())), preferred_element_type=F32
        )
        for b in range(2):
            cols = pl.ds(pl.multiple_of(i * 256 + b * 128, 128), 128)
            inv = invb[...]
            normed = x_v[:, cols].astype(F32) * inv
            ng = pre[:, b * 128 : (b + 1) * 128] * grow[0:1, cols]
            ig_out[:, cols] = (inv * (ng - normed * cb[...])).astype(BF)

    r9()
    rs_last(2, 0)
    rs_y_wait()
    scale = 1.0 / math.sqrt(TOK * 32)
    acc = jnp.zeros((128, 128), F32)
    for k in range(8):
        r = pl.ds(pl.multiple_of(me * KV + k * 128, 128), 128)
        t = ((pt[r, :].astype(F32) + ybuf[k * 128 : (k + 1) * 128, :].astype(F32)) * scale).T
        wg_out[:, k * 128 : (k + 1) * 128] = t
        acc = acc + t * wbuf[pl.ds(own_rows, ROWS), k * 128 : (k + 1) * 128].astype(F32)
    gg_out[...] = jnp.sum(acc.T, axis=0, keepdims=True) / gbuf[me]

    def done(ref, sem):
        remote(ref, ref, sem, g_r.at[0], (rep, ypeer)).wait_send()

    for p in range(PARTS):
        done(wbuf.at[pl.ds(0, 64)], ag_s.at[key_y(p)])
        done(ybuf.at[pl.ds(0, 512)], rs_s.at[key_y(p)])
        for step in range(2):
            for way in range(2):
                keys = [key_1(p, yr, step, way) for yr in range(2)]
                keys += [key_2(p, (yr, o), step, way) for yr in range(2) for o in range(4)]
                for k in keys:
                    done(wbuf.at[pl.ds(0, 32 if step else 64)], ag_s.at[k])
                    done(ybuf.at[pl.ds(0, 512 if step else 256)], rs_s.at[k])
    for k in range(7):
        done(gain_ref(k // 3, 0, 0), g_s.at[k])


def write_kernel(*refs):
    n = len(refs) // 2
    copies = [pltpu.make_async_copy(refs[k], refs[n + k], refs[2 * n].at[k]) for k in range(n)]
    for c in copies:
        c.start()
    for c in copies:
        c.wait()


def local(
    layer_input,
    norm_gain,
    kv_weight,
    kv_cotangent,
    pseudo_grad,
    outer_momentum,
    global_params,
    local_params,
):
    any_spec = pl.BlockSpec(memory_space=pl.ANY)
    vmem = pl.BlockSpec(memory_space=pltpu.VMEM)
    dma = pltpu.SemaphoreType.DMA
    outs = pl.pallas_call(
        kernel,
        out_shape=(
            pltpu.VMEM((TOK, KV), BF),
            pltpu.VMEM((TOK, D), BF),
            pltpu.VMEM((ROWS, KV), F32),
            pltpu.VMEM((1, ROWS), F32),
            pltpu.VMEM((PSR, KV), F32),
            pltpu.VMEM((PSR, KV), F32),
            pltpu.VMEM((PSR, KV), BF),
        ),
        in_specs=[any_spec, vmem] + [any_spec] * 6,
        out_specs=(vmem,) * 7,
        scratch_shapes=[
            pltpu.VMEM((TOK, D), BF),
            pltpu.VMEM((TOK, D), BF),
            pltpu.VMEM((D, KV), BF),
            pltpu.VMEM((TOK, KV), BF),
            pltpu.VMEM((KV, TOK), BF),
            pltpu.VMEM((32 * KV, ROWS), BF),
            pltpu.VMEM((40 * 256, ROWS), BF),
            pltpu.VMEM((40 * 512, ROWS), BF),
            pltpu.VMEM((KV, ROWS), BF),
            pltpu.VMEM((32, 1, ROWS), F32),
            pltpu.VMEM((8, D), F32),
            pltpu.VMEM((TOK, 128), F32),
            pltpu.VMEM((TOK, 128), F32),
            pltpu.VMEM((TOK, 256), F32),
            pltpu.VMEM((TOK, 128), F32),
            pltpu.VMEM((TOK, 128), F32),
            pltpu.VMEM((PSR, KV), F32),
            pltpu.VMEM((PSR // 2, KV), F32),
            pltpu.VMEM((PSR // 2, KV), F32),
            pltpu.VMEM((PSR // 2, KV), F32),
            pltpu.VMEM((PSR // 2, KV), F32),
            pltpu.VMEM((PSR, KV), F32),
            pltpu.VMEM((PSR, KV), F32),
            pltpu.VMEM((PSR, KV), BF),
            dma((10,)),
            dma((2 * PER_PART,)),
            dma((2 * PER_PART,)),
            dma((2 * PER_PART,)),
            dma((2 * PER_PART,)),
            dma((7,)),
            dma((7,)),
            dma((3,)),
            dma((3,)),
        ],
        compiler_params=pltpu.CompilerParams(
            collective_id=0, has_side_effects=True, vmem_limit_bytes=50 * 1024 * 1024
        ),
    )(
        layer_input[0],
        norm_gain,
        kv_weight[0],
        kv_cotangent[0],
        pseudo_grad[0],
        outer_momentum,
        global_params,
        local_params[0],
    )
    outs = pl.pallas_call(
        write_kernel,
        out_shape=tuple(jax.ShapeDtypeStruct(o.shape, o.dtype) for o in outs),
        in_specs=[vmem] * 7,
        out_specs=(any_spec,) * 7,
        scratch_shapes=[dma((7,))],
        compiler_params=pltpu.CompilerParams(vmem_limit_bytes=1024 * 1024),
    )(*outs)
    kv_out, input_grad, weight_grad, gain_grad, momentum_new, global_new, local_new = outs
    return (
        kv_out[None],
        input_grad[None],
        weight_grad[None],
        gain_grad,
        momentum_new,
        global_new,
        local_new[None],
    )


def solution(mesh):
    shared = P("replica", "fsdp", None)
    in_specs = (
        shared,
        P("replica", "fsdp"),
        shared,
        shared,
        shared,
        P("fsdp", None),
        P("fsdp", None),
        shared,
    )
    out_specs = (
        shared,
        shared,
        shared,
        P("replica", "fsdp"),
        P("fsdp", None),
        P("fsdp", None),
        shared,
    )
    return jax.shard_map(local, mesh=mesh, in_specs=in_specs, out_specs=out_specs, check_vma=False)
```

```python
import math

import jax
import jax.numpy as jnp
from jax import lax
from jax.experimental import pallas as pl
from jax.experimental.pallas import tpu as pltpu
from jax.sharding import PartitionSpec as P

HEAD = 128
SEQ_LEN = 4096
D = 4096
KV = 1024
TOK = 512
ROWS = 128
PARTS = 2
PSR = 384

epsilon = 1e-05
rope_base = 500000.0
momentum_rate = 0.9
outer_rate = 0.7
mixing_rate = 0.5

TURN_MID = 507 / 262144
TURN_LOW = 2 * math.pi - 6.28125 - TURN_MID

MESH = pl.DeviceIdType.MESH
BF = jnp.bfloat16
F32 = jnp.float32

SCATTER_ORDER = ((1, 2), (1, 1), (1, 3), (1, 0), (0, 2), (0, 1), (0, 3), (0, 0))
PER_PART = 41


def key_y(p):
    return p * PER_PART


def key_1(p, yr, step, way):
    return p * PER_PART + 1 + yr * 4 + step * 2 + way


def key_2(p, g, step, way):
    return p * PER_PART + 9 + (g[0] * 4 + g[1]) * 4 + step * 2 + way


def turn(angle):
    turns = jnp.round(angle * (0.5 / math.pi))
    angle = ((angle - turns * 6.28125) - turns * TURN_MID) - turns * TURN_LOW
    return jnp.cos(angle), jnp.sin(angle)


def kernel(
    x_hbm,
    gain_v,
    w_hbm,
    ct_hbm,
    ps_hbm,
    om_hbm,
    gp_hbm,
    lp_hbm,
    kv_out,
    ig_out,
    wg_out,
    gg_out,
    mom_out,
    glob_out,
    loc_out,
    x_v,
    hid,
    wbuf,
    kv,
    kvt,
    pt,
    x1,
    x2,
    ybuf,
    gbuf,
    grow,
    invb,
    cb,
    pre,
    cos_v,
    sin_v,
    ps,
    psr,
    psum,
    srecv,
    trecv,
    om,
    gp,
    lp,
    lsem,
    ag_s,
    ag_r,
    rs_s,
    rs_r,
    g_s,
    g_r,
    p_s,
    p_r,
):
    rep = lax.axis_index("replica")
    me = lax.axis_index("fsdp")
    y = me // 16
    zc = (me // 4) % 4
    xc = me % 4
    core = rep % 2

    def at(yr, zo, xo):
        yy = y if yr == 0 else 1 - y
        zz = zc if zo == 0 else (zc + zo) % 4
        xx = xc if xo == 0 else (xc + xo) % 4
        return yy * 16 + zz * 4 + xx

    def shard(p, yr, o1, o2):
        return at(yr, o1, o2) if p == 0 else at(yr, o2, o1)

    shards = {
        (p, yr, o1, o2): shard(p, yr, o1, o2)
        for p in range(PARTS)
        for yr in range(2)
        for o1 in range(4)
        for o2 in range(4)
    }
    ypeer = at(1, 0, 0)
    peers1 = {(p, way): shards[p, 0, 1 if way == 0 else 3, 0] for p in range(PARTS) for way in range(2)}
    peers2 = {(p, way): shards[p, 0, 0, 1 if way == 0 else 3] for p in range(PARTS) for way in range(2)}
    gpeers = [at(0, 0, 1), at(0, 0, 2), at(0, 0, 3), at(0, 1, 0), at(0, 2, 0), at(0, 3, 0), ypeer]
    twin = rep + 1 - 2 * core
    across = (rep + 2) % 4
    half = 192
    mine = pl.multiple_of(core * half, half)
    other = pl.multiple_of((1 - core) * half, half)

    loads = {}

    def load(name, src, dst, k):
        loads[name] = pltpu.make_async_copy(src, dst, lsem.at[k])
        loads[name].start()

    own_rows = pl.multiple_of(me * ROWS, ROWS)
    load("w", w_hbm, wbuf.at[pl.ds(own_rows, ROWS)], 0)
    load("ps", ps_hbm, ps, 2)
    load("ct", ct_hbm, kv, 3)
    load("x", x_hbm, x_v, 6)
    load("om", om_hbm, om, 7)
    load("gp", gp_hbm, gp, 8)
    load("lp", lp_hbm, lp, 9)

    gbuf[me] = gain_v[...].astype(F32)
    barrier = pltpu.get_barrier_semaphore()
    greet = [(rep, d) for d in gpeers] + [(twin, me), (across, me)]
    for dev in greet:
        pl.semaphore_signal(barrier, inc=1, device_id=dev, device_id_type=MESH)
    pl.semaphore_wait(barrier, len(greet))

    sent = []

    def remote(src, dst, ss, rs, dev):
        return pltpu.make_async_remote_copy(
            src_ref=src, dst_ref=dst, send_sem=ss, recv_sem=rs, device_id=dev, device_id_type=MESH
        )

    def wrows(p, s, piece):
        if piece is None:
            return wbuf.at[pl.ds(pl.multiple_of(s * ROWS + p * 64, 64), 64)]
        return wbuf.at[pl.ds(pl.multiple_of(s * ROWS + p * 64 + piece * 32, 32), 32)]

    def ag_send(p, s, piece, k, dev):
        ref = wrows(p, s, piece)
        remote(ref, ref, ag_s.at[k], ag_r.at[k], (rep, dev)).start()

    def ag_wait(p, s, piece, k):
        ref = wrows(p, s, piece)
        remote(ref, ref, ag_s.at[k], ag_r.at[k], (rep, ypeer)).wait_recv()

    def ag_y_send():
        for p in range(PARTS):
            ag_send(p, me, None, key_y(p), ypeer)

    def ag_y_wait():
        for p in range(PARTS):
            ag_wait(p, ypeer, None, key_y(p))

    def ag1_first(yr):
        for p in range(PARTS):
            for way in range(2):
                ag_send(p, shards[p, yr, 0, 0], None, key_1(p, yr, 0, way), peers1[p, way])

    def ag1_next(yr):
        for p in range(PARTS):
            for way in range(2):
                s = shards[p, yr, 3 if way == 0 else 1, 0]
                ag_wait(p, s, None, key_1(p, yr, 0, way))
                ag_send(p, s, way, key_1(p, yr, 1, way), peers1[p, way])

    def ag1_wait(yr):
        for p in range(PARTS):
            for way in range(2):
                ag_wait(p, shards[p, yr, 2, 0], way, key_1(p, yr, 1, way))

    def ag2_first(g):
        for p in range(PARTS):
            for way in range(2):
                ag_send(p, shards[p, g[0], g[1], 0], None, key_2(p, g, 0, way), peers2[p, way])

    def ag2_next(g):
        for p in range(PARTS):
            for way in range(2):
                s = shards[p, g[0], g[1], 3 if way == 0 else 1]
                ag_wait(p, s, None, key_2(p, g, 0, way))
                ag_send(p, s, way, key_2(p, g, 1, way), peers2[p, way])

    def ag2_wait(g):
        for p in range(PARTS):
            for way in range(2):
                ag_wait(p, shards[p, g[0], g[1], 2], way, key_2(p, g, 1, way))

    def prow(p, s, h, n):
        return pl.ds(pl.multiple_of(s * KV + p * 512 + h * 256, 256), n)

    def slot(p, stage, g, way):
        k = (g[0] * 4 + g[1]) if stage == 1 else 8 + g
        return (p * 10 + k) * 2 + way

    def rs_key(p, stage, g, step, way):
        return key_2(p, g, step, way) if stage == 1 else key_1(p, g, step, way)

    def rs_shard(p, stage, g, o):
        return shards[p, g[0], g[1], o] if stage == 1 else shards[p, g, o, 0]

    def rs_peer(p, stage, way):
        return peers2[p, way] if stage == 1 else peers1[p, way]

    def rs_first(stage, g):
        for p in range(PARTS):
            for way in range(2):
                k = rs_key(p, stage, g, 0, way)
                s = slot(p, stage, g, way)
                remote(
                    pt.at[prow(p, rs_shard(p, stage, g, 2), way, 256)],
                    x1.at[pl.ds(s * 256, 256)],
                    rs_s.at[k],
                    rs_r.at[k],
                    (rep, rs_peer(p, stage, way)),
                ).start()

    def rs_next(stage, g):
        for p in range(PARTS):
            for way in range(2):
                k = rs_key(p, stage, g, 0, way)
                s = slot(p, stage, g, way)
                ref = x1.at[pl.ds(s * 256, 256)]
                remote(ref, ref, rs_s.at[k], rs_r.at[k], (rep, ypeer)).wait_recv()
                to = rs_shard(p, stage, g, 1 if way == 0 else 3)
                r = prow(p, to, way, 256)
                pt[r, :] = (pt[r, :].astype(F32) + x1[pl.ds(s * 256, 256), :].astype(F32)).astype(BF)
                k = rs_key(p, stage, g, 1, way)
                remote(
                    pt.at[prow(p, to, 0, 512)],
                    x2.at[pl.ds(s * 512, 512)],
                    rs_s.at[k],
                    rs_r.at[k],
                    (rep, rs_peer(p, stage, way)),
                ).start()

    def rs_last(stage, g):
        for p in range(PARTS):
            for way in range(2):
                k = rs_key(p, stage, g, 1, way)
                ref = x2.at[pl.ds(slot(p, stage, g, way) * 512, 512)]
                remote(ref, ref, rs_s.at[k], rs_r.at[k], (rep, ypeer)).wait_recv()
            r = prow(p, rs_shard(p, stage, g, 0), 0, 512)
            a = x2[pl.ds(slot(p, stage, g, 0) * 512, 512), :].astype(F32)
            b = x2[pl.ds(slot(p, stage, g, 1) * 512, 512), :].astype(F32)
            pt[r, :] = (pt[r, :].astype(F32) + (a + b)).astype(BF)

    def rs_y_send():
        for p in range(PARTS):
            k = key_y(p)
            remote(
                pt.at[prow(p, ypeer, 0, 512)],
                ybuf.at[pl.ds(p * 512, 512)],
                rs_s.at[k],
                rs_r.at[k],
                (rep, ypeer),
            ).start()

    def rs_y_wait():
        for p in range(PARTS):
            k = key_y(p)
            ref = ybuf.at[pl.ds(p * 512, 512)]
            remote(ref, ref, rs_s.at[k], rs_r.at[k], (rep, ypeer)).wait_recv()

    def gain_ref(stage, yr, off):
        if stage == 0:
            return gbuf.at[at(yr, 0, off)]
        if stage == 1:
            return gbuf.at[pl.ds(at(yr, off, 0) // 4 * 4, 4)]
        return gbuf.at[pl.ds(at(yr, 0, 0) // 16 * 16, 16)]

    def gain_send(stage):
        for o in (1, 2, 3) if stage < 2 else (0,):
            k = stage * 3 + max(o, 1) - 1
            ref = gain_ref(stage, 0, 0)
            remote(ref, ref, g_s.at[k], g_r.at[k], (rep, gpeers[k])).start()

    def gain_wait(stage):
        for o in (1, 2, 3) if stage < 2 else (0,):
            k = stage * 3 + max(o, 1) - 1
            ref = gain_ref(stage, 0, 4 - o) if stage < 2 else gain_ref(2, 1, 0)
            remote(ref, ref, g_s.at[k], g_r.at[k], (rep, ypeer)).wait_recv()

    def ps_send(k):
        if k == 0:
            src, dst, dev = ps.at[pl.ds(other, half)], psr, (twin, me)
        elif k == 1:
            src, dst, dev = psum, srecv, (across, me)
        else:
            src, dst, dev = ps.at[pl.ds(mine, half)], trecv, (twin, me)
        remote(src, dst, p_s.at[k], p_r.at[k], dev).start()

    def ps_wait(k):
        ref = (psr, srecv, trecv)[k]
        remote(ref, ref, p_s.at[k], p_r.at[k], (twin, me)).wait_recv()

    def ps_sent(k):
        ref = (psr, srecv, trecv)[k]
        remote(ref, ref, p_s.at[k], p_r.at[k], (twin, me)).wait_send()

    loads["w"].wait()
    gain_send(0)
    ag1_first(0)
    ag_y_send()
    loads["ps"].wait()
    ps_send(0)

    lane = lax.broadcasted_iota(jnp.int32, (64, HEAD), 1)
    inverse = jnp.exp((lane % (HEAD // 2)).astype(F32) * (-2.0 * math.log(rope_base) / HEAD))
    small = lax.broadcasted_iota(jnp.int32, (64, HEAD), 0).astype(F32) * inverse
    position = (me * TOK) % SEQ_LEN + 64 * lax.broadcasted_iota(jnp.int32, (8, HEAD), 0)
    base = position.astype(F32) * inverse[:8]
    cos_0, sin_0 = turn(small)
    cos_b, sin_b = turn(base)
    sign = jnp.where(lane < HEAD // 2, -1.0, 1.0)
    for b in range(8):
        cb_row, sb_row = cos_b[b : b + 1], sin_b[b : b + 1]
        cos_v[b * 64 : (b + 1) * 64, :] = cos_0 * cb_row - sin_0 * sb_row
        sin_v[b * 64 : (b + 1) * 64, :] = (sin_0 * cb_row + cos_0 * sb_row) * sign

    gain_wait(0)
    gain_send(1)
    ag2_first((0, 0))

    loads["ct"].wait()

    @pl.loop(0, 4)
    def _(h):
        cols = pl.ds(pl.multiple_of(h * HEAD, HEAD), HEAD)
        v = kv[:, cols].astype(F32)
        r = (v * cos_v[...] - pltpu.roll(v, HEAD // 2, 1) * sin_v[...]).astype(BF)
        kv[:, cols] = r
        kvt[cols, :] = r.T

    ag1_next(0)
    ag2_first((0, 3))
    ag2_first((0, 1))

    @pl.loop(4, 8)
    def _(h):
        cols = pl.ds(pl.multiple_of(h * HEAD, HEAD), HEAD)
        kvt[cols, :] = kv[:, cols].T

    gain_wait(1)
    gain_send(2)
    ag_y_wait()
    ag1_first(1)
    ag2_next((0, 0))
    ag1_wait(0)
    ag2_first((1, 0))
    ag2_first((0, 2))

    ps_wait(0)
    ps_sent(0)

    @pl.loop(0, 4)
    def _(i):
        r = pl.ds(pl.multiple_of(i * 48, 16), 48)
        rm = pl.ds(pl.multiple_of(mine + i * 48, 16), 48)
        psum[r, :] = (ps[rm, :] + psr[r, :]).astype(BF)

    gain_wait(2)
    ps_send(1)
    for j in range(32):
        grow[:, j * 128 : (j + 1) * 128] = jnp.broadcast_to(gbuf[j], (8, 128))
    loads["x"].wait()

    @pl.loop(0, TOK // 64)
    def _(i):
        r = pl.ds(pl.multiple_of(i * 64, 64), 64)
        acc = jnp.zeros((64, 128), F32)
        for k in range(D // 128):
            v = x_v[r, k * 128 : (k + 1) * 128].astype(F32)
            acc = acc + v * v
        inv = lax.rsqrt(jnp.sum(acc, axis=-1, keepdims=True) * (1.0 / D) + epsilon)
        invb[r, :] = jnp.broadcast_to(inv, (64, 128))

    def ag_a():
        ag2_next((0, 3))

    def ag_b():
        ag2_next((0, 1))

    def ag_c():
        ag1_next(1)
        ag2_first((1, 3))
        ag2_first((1, 1))

    hidden_steps = {4: ag_a, 12: ag_b, 28: ag_c}

    @pl.loop(0, TOK // 16)
    def _(i):
        for k, fn in hidden_steps.items():
            pl.when(i == k)(fn)
        r = pl.ds(pl.multiple_of(i * 16, 16), 16)
        inv = invb[r, :]
        for k in range(D // 128):
            c = slice(k * 128, (k + 1) * 128)
            v = x_v[r, c].astype(F32) * inv
            hid[r, c] = (v.reshape(2, 8, 128) * grow[:, c][None]).reshape(16, 128).astype(BF)

    def ag_d():
        ag2_next((1, 0))

    def ag_e():
        ag2_next((0, 2))
        ag1_wait(1)
        ag2_first((1, 2))

    steps = {4: ag_d, 11: ag_e}

    @pl.loop(0, 16)
    def _(i):
        for k, fn in steps.items():
            pl.when(i == k)(fn)
        res = jnp.dot(
            kvt[...],
            hid[:, pl.ds(pl.multiple_of(i * 256, 256), 256)],
            preferred_element_type=F32,
        )
        r0 = pl.multiple_of(i * 2048, 2048)
        pt[pl.ds(r0, 1024), :] = res[:, :128].astype(BF)
        pt[pl.ds(r0 + 1024, 1024), :] = res[:, 128:].astype(BF)

    order = SCATTER_ORDER
    ag2_next((1, 3))
    ag2_next((1, 1))
    rs_first(1, order[0])
    rs_first(1, order[1])
    ag2_next((1, 2))
    for yr in range(2):
        for o in range(4):
            ag2_wait((yr, o))

    def r0():
        rs_first(1, order[2])
        rs_next(1, order[0])

    def r1():
        rs_first(1, order[3])
        rs_next(1, order[1])

    def r2():
        rs_first(1, order[4])
        rs_next(1, order[2])

    def r2b():
        rs_last(1, order[0])
        rs_first(2, 1)

    def r3():
        rs_first(1, order[5])
        rs_next(1, order[3])
        rs_last(1, order[1])

    def r4():
        rs_first(1, order[6])
        rs_next(1, order[4])

    def r4b():
        rs_last(1, order[2])
        rs_next(2, 1)

    def r5():
        rs_first(1, order[7])
        rs_next(1, order[5])
        rs_last(1, order[3])

    def r6():
        rs_next(1, order[6])
        rs_last(1, order[4])
        rs_first(2, 0)

    def r6b():
        rs_last(2, 1)
        rs_y_send()

    def r7():
        rs_next(1, order[7])
        rs_last(1, order[5])

    def r8():
        rs_last(1, order[6])
        rs_next(2, 0)

    def r9():
        rs_last(1, order[7])

    cb[...] = jnp.zeros_like(cb)
    fwd_steps = {0: r0, 1: r1, 2: r2, 3: r2b}

    @pl.loop(0, 4)
    def _(n):
        for k, fn in fwd_steps.items():
            pl.when(n == k)(fn)
        cols = pl.ds(pl.multiple_of(n * 256, 256), 256)
        pre[...] = jnp.dot(hid[...], wbuf[:, cols], preferred_element_type=F32)
        for b in range(2):
            c128 = pl.ds(pl.multiple_of(n * 256 + b * 128, 128), 128)
            v = pre[:, b * 128 : (b + 1) * 128]
            cb[...] += v * kv[:, c128].astype(F32)

            @pl.when(n < 2)
            def _():
                v = pre[:, b * 128 : (b + 1) * 128]
                kv_out[:, c128] = (v * cos_v[...] + pltpu.roll(v, HEAD // 2, 1) * sin_v[...]).astype(BF)

            @pl.when(n >= 2)
            def _():
                kv_out[:, c128] = pre[:, b * 128 : (b + 1) * 128].astype(BF)

    cb[...] = jnp.broadcast_to(jnp.sum(cb[...], axis=-1, keepdims=True) * (1.0 / D), (TOK, 128))

    ps_wait(1)
    ps_sent(1)

    @pl.loop(0, 4)
    def _(i):
        r = pl.ds(pl.multiple_of(i * 48, 16), 48)
        rm = pl.ds(pl.multiple_of(mine + i * 48, 16), 48)
        ps[rm, :] = psum[r, :].astype(F32) + srecv[r, :].astype(F32)

    ps_send(2)

    bwd_steps = {0: r3, 2: r4, 4: r4b, 5: r5, 8: r6, 10: r6b, 12: r7, 15: r8}

    @pl.loop(0, 16)
    def _(i):
        for k, fn in bwd_steps.items():
            pl.when(i == k)(fn)
        rows = pl.ds(pl.multiple_of(i * 256, 256), 256)
        pre[...] = lax.dot_general(
            kv[...], wbuf[rows, :], (((1,), (1,)), ((), ())), preferred_element_type=F32
        )
        for b in range(2):
            cols = pl.ds(pl.multiple_of(i * 256 + b * 128, 128), 128)
            inv = invb[...]
            normed = x_v[:, cols].astype(F32) * inv
            ng = pre[:, b * 128 : (b + 1) * 128] * grow[0:1, cols]
            ig_out[:, cols] = (inv * (ng - normed * cb[...])).astype(BF)

    r9()
    ps_wait(2)
    ps_sent(2)
    loads["om"].wait()
    loads["gp"].wait()
    loads["lp"].wait()

    def update(r, total):
        average = total * 0.25
        m = momentum_rate * om[r, :] + average
        gn = gp[r, :] - outer_rate * (average + momentum_rate * m)
        mom_out[r, :] = m
        glob_out[r, :] = gn
        loc_out[r, :] = (mixing_rate * lp[r, :].astype(F32) + (1.0 - mixing_rate) * gn).astype(BF)

    @pl.loop(0, 12)
    def _(i):
        rm = pl.ds(pl.multiple_of(mine + i * 16, 16), 16)
        update(rm, ps[rm, :])
        ro = pl.ds(pl.multiple_of(other + i * 16, 16), 16)
        update(ro, trecv[pl.ds(pl.multiple_of(i * 16, 16), 16), :])

    rs_last(2, 0)
    rs_y_wait()
    scale = 1.0 / math.sqrt(TOK * 32)
    acc = jnp.zeros((128, 128), F32)
    for k in range(8):
        r = pl.ds(pl.multiple_of(me * KV + k * 128, 128), 128)
        t = ((pt[r, :].astype(F32) + ybuf[k * 128 : (k + 1) * 128, :].astype(F32)) * scale).T
        wg_out[:, k * 128 : (k + 1) * 128] = t
        acc = acc + t * wbuf[pl.ds(own_rows, ROWS), k * 128 : (k + 1) * 128].astype(F32)
    gg_out[...] = jnp.sum(acc.T, axis=0, keepdims=True) / gbuf[me]

    def done(ref, sem):
        remote(ref, ref, sem, g_r.at[0], (rep, ypeer)).wait_send()

    for p in range(PARTS):
        done(wbuf.at[pl.ds(0, 64)], ag_s.at[key_y(p)])
        done(ybuf.at[pl.ds(0, 512)], rs_s.at[key_y(p)])
        for step in range(2):
            for way in range(2):
                keys = [key_1(p, yr, step, way) for yr in range(2)]
                keys += [key_2(p, (yr, o), step, way) for yr in range(2) for o in range(4)]
                for k in keys:
                    done(wbuf.at[pl.ds(0, 32 if step else 64)], ag_s.at[k])
                    done(ybuf.at[pl.ds(0, 512 if step else 256)], rs_s.at[k])
    for k in range(7):
        done(gain_ref(k // 3, 0, 0), g_s.at[k])


def write_kernel(*refs):
    n = len(refs) // 2
    copies = [pltpu.make_async_copy(refs[k], refs[n + k], refs[2 * n].at[k]) for k in range(n)]
    for c in copies:
        c.start()
    for c in copies:
        c.wait()


def local(
    layer_input,
    norm_gain,
    kv_weight,
    kv_cotangent,
    pseudo_grad,
    outer_momentum,
    global_params,
    local_params,
):
    any_spec = pl.BlockSpec(memory_space=pl.ANY)
    vmem = pl.BlockSpec(memory_space=pltpu.VMEM)
    dma = pltpu.SemaphoreType.DMA
    outs = pl.pallas_call(
        kernel,
        out_shape=(
            pltpu.VMEM((TOK, KV), BF),
            pltpu.VMEM((TOK, D), BF),
            pltpu.VMEM((ROWS, KV), F32),
            pltpu.VMEM((1, ROWS), F32),
            pltpu.VMEM((PSR, KV), F32),
            pltpu.VMEM((PSR, KV), F32),
            pltpu.VMEM((PSR, KV), BF),
        ),
        in_specs=[any_spec, vmem] + [any_spec] * 6,
        out_specs=(vmem,) * 7,
        scratch_shapes=[
            pltpu.VMEM((TOK, D), BF),
            pltpu.VMEM((TOK, D), BF),
            pltpu.VMEM((D, KV), BF),
            pltpu.VMEM((TOK, KV), BF),
            pltpu.VMEM((KV, TOK), BF),
            pltpu.VMEM((32 * KV, ROWS), BF),
            pltpu.VMEM((40 * 256, ROWS), BF),
            pltpu.VMEM((40 * 512, ROWS), BF),
            pltpu.VMEM((KV, ROWS), BF),
            pltpu.VMEM((32, 1, ROWS), F32),
            pltpu.VMEM((8, D), F32),
            pltpu.VMEM((TOK, 128), F32),
            pltpu.VMEM((TOK, 128), F32),
            pltpu.VMEM((TOK, 256), F32),
            pltpu.VMEM((TOK, 128), F32),
            pltpu.VMEM((TOK, 128), F32),
            pltpu.VMEM((PSR, KV), F32),
            pltpu.VMEM((PSR // 2, KV), F32),
            pltpu.VMEM((PSR // 2, KV), BF),
            pltpu.VMEM((PSR // 2, KV), BF),
            pltpu.VMEM((PSR // 2, KV), F32),
            pltpu.VMEM((PSR, KV), F32),
            pltpu.VMEM((PSR, KV), F32),
            pltpu.VMEM((PSR, KV), BF),
            dma((10,)),
            dma((2 * PER_PART,)),
            dma((2 * PER_PART,)),
            dma((2 * PER_PART,)),
            dma((2 * PER_PART,)),
            dma((7,)),
            dma((7,)),
            dma((3,)),
            dma((3,)),
        ],
        compiler_params=pltpu.CompilerParams(
            collective_id=0, has_side_effects=True, vmem_limit_bytes=50 * 1024 * 1024
        ),
    )(
        layer_input[0],
        norm_gain,
        kv_weight[0],
        kv_cotangent[0],
        pseudo_grad[0],
        outer_momentum,
        global_params,
        local_params[0],
    )
    outs = pl.pallas_call(
        write_kernel,
        out_shape=tuple(jax.ShapeDtypeStruct(o.shape, o.dtype) for o in outs),
        in_specs=[vmem] * 7,
        out_specs=(any_spec,) * 7,
        scratch_shapes=[dma((7,))],
        compiler_params=pltpu.CompilerParams(vmem_limit_bytes=1024 * 1024),
    )(*outs)
    kv_out, input_grad, weight_grad, gain_grad, momentum_new, global_new, local_new = outs
    return (
        kv_out[None],
        input_grad[None],
        weight_grad[None],
        gain_grad,
        momentum_new,
        global_new,
        local_new[None],
    )


def solution(mesh):
    shared = P("replica", "fsdp", None)
    in_specs = (
        shared,
        P("replica", "fsdp"),
        shared,
        shared,
        shared,
        P("fsdp", None),
        P("fsdp", None),
        shared,
    )
    out_specs = (
        shared,
        shared,
        shared,
        P("replica", "fsdp"),
        P("fsdp", None),
        P("fsdp", None),
        shared,
    )
    return jax.shard_map(local, mesh=mesh, in_specs=in_specs, out_specs=out_specs, check_vma=False)
```
